512 devices in a mesh: branch: 2 (over y_hi), ctx: 32 (over x, y_lo, core), tp: 8 (over z).
Axes of the slice: x: 4, y: 8 (y_hi: 2, y_lo: 4; y = y_hi * 4 + y_lo), z: 8, core: 2. Of those that a mesh axis runs over, the one named last changes fastest.
Arguments:
- queries: bfloat16 [2, 8192, 8192], P('branch', 'ctx', 'tp'), may hold values from -12 to 12
- keys: bfloat16 [2, 8192, 1024], P('branch', 'ctx', 'tp'), may hold values from -12 to 12
- values: bfloat16 [2, 8192, 1024], P('branch', 'ctx', 'tp'), may hold values from -800 to 800
- segments: int32 [8192], replicated, may hold values from 0 to 3, never falling along the last dimension, each value on 1 to 4096 neighbouring positions
- norm_gain: float32 [2, 8192], P('branch', 'tp'), may hold values from 0.5 to 1.5
- head_weight: float32 [2, 8192], P('branch', 'tp'), may hold values from -0.0625 to 0.0625
Outputs:
- normed: bfloat16 [2, 8192, 8192], P('branch', 'ctx', 'tp')
- joined: float32 [8192], P('ctx')
The draws below stay inside these ranges and needn't reach their ends.
Inputs may be any that keep to these rules, and one draw needn't show every extreme that they name: `segments`: rollout ids never fall along the sequence; each rollout holds 1 to 4096 tokens, and one holds exactly 4096.
All inputs are finite; a program needn't handle non-finite values.
Results may differ from the reference program's by a relative error of at most 0.007.
Values may be sent and summed in bfloat16 or wider, within the bound.
No kernel may reach another device: no remote copies, remote signals or barrier semaphores. Data moves between devices by JAX's collectives and lax.ppermute only.
A program may use at most 64 MiB of HBM per device.

```python
import math
import jax
import jax.numpy as jnp
import numpy as np
from jax import lax

H = 64
KVH = 8
HD = 128
COUNT = 4
D = 8192
L = 8192
MOST = 4096


def draw_queries(key, part):
    noise_key = jax.random.fold_in(key, 11)
    drawn = jnp.clip(jax.random.normal(noise_key, (2, L, D), jnp.float32), -4.0, 4.0)
    return drawn.astype(jnp.bfloat16)


def draw_keys(key, part):
    noise_key = jax.random.fold_in(key, 17)
    drawn = jnp.clip(jax.random.normal(noise_key, (2, L, KVH * HD), jnp.float32), -4.0, 4.0)
    return drawn.astype(jnp.bfloat16)


def draw_values(key, part):
    noise_key, column_key, row_key = jax.random.split(jax.random.fold_in(key, 31), 3)
    columns = KVH * HD
    head_number = (jnp.arange(columns) // HD).astype(jnp.float32)
    drawn = jnp.clip(jax.random.normal(noise_key, (2, L, columns), jnp.float32), -4.0, 4.0)
    rising = 1.0 + head_number / max(KVH - 1, 1)
    column_scale = jnp.exp(jax.random.uniform(column_key, (2, 1, columns), jnp.float32) * math.log(10.0))
    row_scale = jnp.exp(jax.random.uniform(row_key, (2, L, 1), jnp.float32) * math.log(10.0))
    return (drawn * rising * column_scale * row_scale).astype(jnp.bfloat16)


def block_scale(own_key, extent, cuts, low, largest):
    def one(axis_at, parts):
        heights = jax.random.uniform(jax.random.fold_in(jax.random.fold_in(own_key, 6), axis_at), (parts,), jnp.float32, low / len(cuts), largest / len(cuts))
        return jnp.repeat(jnp.exp(heights), extent[axis_at] // parts).reshape((-1,) + (1,) * (len(extent) - axis_at - 1))

    loudness = one(*cuts[0])
    for cut in cuts[1:]:
        loudness = loudness * one(*cut)
    return loudness


def profile(count, total, limit, lean):
    portions = [(1 << 20) // math.isqrt(grade ** lean) + 1 for grade in range(2, count + 1)]
    rest, holding = total - limit - (count - 1), [1] * (count - 1)
    while rest > 0:
        candidates = [i for i in range(count - 1) if holding[i] < limit]
        whole, left = sum([portions[i] for i in candidates]), rest
        for i in candidates:
            extra = min(limit - holding[i], max(1, left * portions[i] // whole), rest)
            holding[i] = holding[i] + extra
            rest = rest - extra
    return np.array([limit] + holding)


def uneven_parts(own_key, count, total, reach, slope):
    if count == 2:
        one = jax.random.randint(own_key, (), max(1, total - reach), min(reach, total - 1) + 1)
        return jnp.stack([one, total - one])
    tallies = jnp.asarray(profile(count, total, reach, slope), jnp.int32)
    twos = (count - 1) // 2
    giver, sink = tallies[1:1 + 2 * twos:2], tallies[2:2 + 2 * twos:2]
    room = jnp.minimum(giver - 1, reach - sink)
    passed = jax.random.randint(jax.random.fold_in(own_key, 1), (twos,), 0, 1 << 20) % (room + 1)
    tallies = tallies.at[1:1 + 2 * twos:2].set(giver - passed).at[2:2 + 2 * twos:2].set(sink + passed)
    return tallies[jax.random.permutation(jax.random.fold_in(own_key, 2), count)]


def scatter_about(key, shape, scale, bound, shards=(), kind=jnp.bfloat16):
    level = block_scale(key, shape, shards, -0.22, 0.18) if shards else 1.0
    values = jax.random.normal(key, shape, jnp.float32) * scale * level
    return jnp.minimum(jnp.maximum(values, -bound), bound).astype(kind)


def setup_inputs(seed: int = 0) -> dict:
    key_of = jax.random.split(jax.random.key(seed), 7)
    return {
        "queries": draw_queries(jax.random.fold_in(key_of[6], 71), 0),
        "keys": draw_keys(jax.random.fold_in(key_of[6], 71), 0),
        "values": draw_values(jax.random.fold_in(key_of[6], 71), 0),
        "segments": jnp.searchsorted(jnp.cumsum(uneven_parts(key_of[3], COUNT, L, MOST, 1)), jnp.arange(L), side="right").astype(jnp.int32),
        "norm_gain": jnp.clip(1.0 + 0.1 * jax.random.normal(key_of[4], (2, D), jnp.float32), 0.5, 1.5),
        "head_weight": scatter_about(key_of[5], (2, D), D ** -0.5, 0.0625, ((0, 2), (1, 8)), jnp.float32),
    }


NEGATIVE = -1e+30
EPSILON = 1e-06

def attend(queries, keys, values, segments):
    per_group = H // KVH
    block_rows = min(L, 256)
    query_heads = queries.astype(jnp.float32).reshape(L, KVH, per_group, HD)
    key_heads = keys.astype(jnp.float32).reshape(L, KVH, HD)
    value_heads = values.astype(jnp.float32).reshape(L, KVH, HD)
    positions = jnp.arange(L, dtype=jnp.int32)

    def visit_block(number):
        begin = (number * block_rows).astype(jnp.int32)
        query_block = lax.dynamic_slice_in_dim(query_heads, begin, block_rows, 0)
        query_pos = begin + jnp.arange(block_rows, dtype=jnp.int32)
        query_seg = lax.dynamic_slice_in_dim(segments, begin, block_rows, 0)
        scores = jnp.einsum('tkgd,pkd->kgtp', query_block, key_heads) * (1.0 / math.sqrt(HD))
        allowed = (segments[None, :] == query_seg[:, None]) & (positions[None, :] <= query_pos[:, None])
        scores = jnp.where(allowed, scores, NEGATIVE)
        maxima = lax.optimization_barrier(jnp.max(scores, axis=-1, keepdims=True))
        weights = jnp.where(allowed, jnp.exp(scores - maxima), 0.0)
        totals = lax.optimization_barrier(jnp.sum(weights, axis=-1))
        rounded = lax.optimization_barrier(weights.astype(jnp.bfloat16)).astype(jnp.float32)
        mixed = jnp.einsum('kgtp,pkd->tkgd', rounded, value_heads)
        mixed = mixed / jnp.transpose(totals, (2, 0, 1))[..., None]
        return mixed.reshape(block_rows, D).astype(jnp.bfloat16)
    blocks = lax.map(visit_block, jnp.arange(L // block_rows, dtype=jnp.int32))
    return blocks.reshape(L, D)

def reference(queries, keys, values, segments, norm_gain, head_weight):
    normed_list = []
    score_list = []
    for section in range(2):
        attn_rows = attend(queries[section], keys[section], values[section], segments)
        attended = lax.optimization_barrier(attn_rows).astype(jnp.float32)
        inverse = lax.rsqrt(lax.optimization_barrier(jnp.mean(attended * attended, axis=-1)) + EPSILON)
        scaled = attended * inverse[:, None] * norm_gain[section].astype(jnp.float32)
        normed_list.append(scaled.astype(jnp.bfloat16))
        score_list.append(lax.optimization_barrier(jnp.sum(scaled * head_weight[section].astype(jnp.float32), axis=-1)))
    return (jnp.stack(normed_list), score_list[0] + score_list[1])
```

```python
import functools
import math

import jax
import jax.numpy as jnp
from jax import lax
from jax.experimental import pallas as pl
from jax.experimental.pallas import tpu as pltpu
from jax.sharding import PartitionSpec as P

H = 64
KVH = 8
HD = 128
D = 8192
NEGATIVE = -1e30
EPSILON = 1e-06

NX, NY = 4, 4
TOGETHER = 2


def unpack(d):
    return d // (2 * NY), (d // 2) % NY, d % 2


def pack(x, y, core):
    return (x * NY + y) * 2 + core


def moved(block, target):
    route = []
    for d in range(2 * NX * NY):
        x, y, core = target(*unpack(d))
        if 0 <= x < NX and 0 <= y < NY:
            route.append((d, pack(x, y, core)))
    return lax.ppermute(block, "ctx", route)


def attend_kernel(first, last, counts, *refs):
    meta, q_ref, starts_ref = refs[:3]
    refs = refs[3:]
    kv_refs, refs = refs[: len(counts)], refs[len(counts) :]
    if not first:
        (m_in, l_in, acc_in), refs = refs[:3], refs[3:]
    if last:
        gain_ref, weight_ref = refs[:2]
        refs = refs[2:]
        att_ref, stats_ref, m_ref, l_ref, acc_ref, sq_ref, dot_ref = refs
    else:
        m_ref, l_ref, acc_ref = refs
    rows = q_ref.shape[0]
    keys = kv_refs[0].shape[2]
    together = q_ref.shape[1] // HD
    factor = math.log2(math.e) / math.sqrt(HD)

    if first:
        m_ref[...] = jnp.full_like(m_ref, NEGATIVE)
        l_ref[...] = jnp.zeros_like(l_ref)
        acc_ref[...] = jnp.zeros_like(acc_ref)
    else:
        m_ref[...] = m_in[...]
        l_ref[...] = l_in[...]
        acc_ref[...] = acc_in[...]

    def visit(key_rows, value_rows, offset, masked):
        if masked:
            key_pos = offset + lax.broadcasted_iota(jnp.int32, (rows, keys), 1)
            query_pos = meta[0] + lax.broadcasted_iota(jnp.int32, (rows, keys), 0)
            allowed = (key_pos >= starts_ref[...]) & (key_pos <= query_pos)
        for g in range(together):
            at = slice(g * HD, (g + 1) * HD)
            scores = lax.dot_general(
                q_ref[:, at], key_rows, (((1,), (1,)), ((), ())), preferred_element_type=jnp.float32
            )
            if masked:
                scores = jnp.where(allowed, scores, NEGATIVE)
            old = m_ref[:, at]
            new = jnp.maximum(old, jnp.max(scores, axis=1, keepdims=True))
            rescale = jnp.exp2((old - new) * factor)
            shift = new * factor
            weights = jnp.exp2(scores * factor - jnp.concatenate([shift] * (keys // HD), axis=1))
            part = weights[:, :HD]
            for c in range(1, keys // HD):
                part = part + weights[:, c * HD : (c + 1) * HD]
            m_ref[:, at] = new
            l_ref[:, at] = l_ref[:, at] * rescale + part
            mixed = jnp.dot(
                weights.astype(jnp.bfloat16), value_rows, preferred_element_type=jnp.float32
            )
            acc_ref[:, at] = acc_ref[:, at] * rescale + mixed

    base = 0
    for kv_ref, count in zip(kv_refs, counts):

        def one(j, carry, kv_ref=kv_ref, base=base):
            offset = meta[1 + 2 * (base + j)]
            kind = meta[2 + 2 * (base + j)]

            @pl.when(kind == 1)
            def _():
                visit(kv_ref[j, 0], kv_ref[j, 1], offset, False)

            @pl.when(kind == 2)
            def _():
                visit(kv_ref[j, 0], kv_ref[j, 1], offset, True)

            return carry

        lax.fori_loop(0, count, one, 0)
        base += count

    if last:
        step = pl.program_id(0)

        @pl.when(step == 0)
        def _():
            sq_ref[...] = jnp.zeros_like(sq_ref)
            dot_ref[...] = jnp.zeros_like(dot_ref)

        for g in range(together):
            at = slice(g * HD, (g + 1) * HD)
            total = jnp.sum(l_ref[:, at], axis=1, keepdims=True)
            attended = (acc_ref[:, at] / total).astype(jnp.bfloat16)
            att_ref[:, at] = attended
            wide = attended.astype(jnp.float32)
            sq_ref[...] += wide * wide
            dot_ref[...] += wide * gain_ref[:, at] * weight_ref[:, at]

        @pl.when(step == pl.num_programs(0) - 1)
        def _():
            ones = jnp.ones((8, HD), jnp.float32)
            for n, ref in enumerate((sq_ref, dot_ref)):
                line = lax.dot_general(
                    ones,
                    ref[...],
                    (((1,), (1,)), ((), ())),
                    precision=lax.Precision.HIGHEST,
                    preferred_element_type=jnp.float32,
                )[:1]
                stats_ref[:, n, :] = jnp.broadcast_to(line, (stats_ref.shape[0], rows))


def attend(meta, queries, starts, blocks, state=None, finish=None, copies=1):
    rows, width = queries.shape
    first, last = state is None, finish is not None
    counts = tuple(b.shape[0] for b in blocks)
    wide = TOGETHER * HD
    column = pl.BlockSpec((rows, wide), lambda h, meta: (0, h))
    whole = lambda a: pl.BlockSpec(a.shape, lambda h, meta: (0,) * a.ndim)
    line = pl.BlockSpec((1, wide), lambda h, meta: (0, h))
    operands = [queries, starts, *blocks]
    in_specs = [column, whole(starts), *[whole(b) for b in blocks]]
    if not first:
        operands += list(state)
        in_specs += [column] * 3
    full = jax.ShapeDtypeStruct((rows, width), jnp.float32)
    scratch = []
    if last:
        operands += list(finish)
        in_specs += [line] * 2
        out_shape = (
            jax.ShapeDtypeStruct((rows, width), jnp.bfloat16),
            jax.ShapeDtypeStruct((copies, 2, rows), jnp.float32),
        )
        out_specs = (column, pl.BlockSpec((copies, 2, rows), lambda h, meta: (0, 0, 0)))
        scratch = [pltpu.VMEM((rows, wide), jnp.float32)] * 3 + [
            pltpu.VMEM((rows, HD), jnp.float32)
        ] * 2
    else:
        out_shape = (full,) * 3
        out_specs = (column,) * 3
    keys = blocks[0].shape[2]
    pairs = sum(counts) * keys * rows * (width // HD)
    return pl.pallas_call(
        functools.partial(attend_kernel, first, last, counts),
        out_shape=out_shape,
        grid_spec=pltpu.PrefetchScalarGridSpec(
            num_scalar_prefetch=1,
            grid=(width // wide,),
            in_specs=in_specs,
            out_specs=out_specs,
            scratch_shapes=scratch,
        ),
        compiler_params=pltpu.CompilerParams(dimension_semantics=("arbitrary",)),
        cost_estimate=pl.CostEstimate(
            flops=4 * pairs * HD, bytes_accessed=8 * rows * width, transcendentals=pairs
        ),
        name="attend",
    )(meta, *operands)


def local(queries, keys, values, segments, norm_gain, head_weight):
    rows = queries.shape[1]
    here = lax.axis_index("ctx")
    x, y, core = unpack(here)
    first_row = here * rows

    below = jnp.sum(
        segments[None, :] < jnp.arange(4, dtype=jnp.int32)[:, None], axis=1, dtype=jnp.int32
    )
    seg_query = lax.dynamic_slice_in_dim(segments, first_row, rows, 0)
    starts = jnp.zeros_like(seg_query)
    for s in range(1, 4):
        starts = jnp.where(seg_query == s, below[s], starts)
    low, high = starts[0], starts[rows - 1]

    def table(places):
        entries = [first_row]
        for xx, yy, cc in places:
            offset = pack(xx, yy, cc) * rows
            valid = (xx >= 0) & (offset <= first_row) & (offset + rows > low)
            clear = (offset >= high) & (offset + rows <= first_row)
            entries += [offset, jnp.where(valid, jnp.where(clear, 1, 2), 0)]
        return jnp.stack([jnp.asarray(e, jnp.int32) for e in entries])

    own = jnp.stack([keys[0], values[0]])[None]
    from_1 = moved(own, lambda x, y, c: (x + 1, y, c))
    from_2 = moved(own, lambda x, y, c: (x + 2, y, c))
    column = jnp.concatenate([from_2, from_1, own])

    rises_2 = (y < 2).astype(jnp.int32)
    rises_1 = 1 - y % 2
    pick = lambda up: lax.dynamic_slice_in_dim(column, up, 2, 0)
    across_2 = moved(pick(rises_2), lambda x, y, c: (x, y ^ 2, c))
    across_1 = moved(pick(rises_1), lambda x, y, c: (x, y ^ 1, c))
    partner = lambda b: moved(b, lambda x, y, c: (x, y, c ^ 1))
    column_p = partner(column)
    across_3 = moved(across_2, lambda x, y, c: (x, y ^ 1, c))
    across_1p, across_2p = partner(across_1), partner(across_2)
    across_3p = partner(across_3)

    def pair(yy, c):
        top = jnp.where(yy < y, x, x - 1)
        return [(top - 1, yy, c), (top, yy, c)]

    y1, y2, y3 = y ^ 1, y ^ 2, y ^ 3
    other = 1 - core
    q = queries[0]
    start_column = starts[:, None]
    places_a = [(x, y, core)] + [(x - 2, y, core), (x - 1, y, core)]
    places_a += [(x - 2, y, other), (x - 1, y, other), (x, y, other)]
    state = attend(
        table(places_a), q, start_column, [own, from_2, from_1, column_p]
    )
    state = attend(
        table(pair(y1, core) + pair(y2, core) + pair(y1, other) + pair(y2, other)),
        q,
        start_column,
        [across_1, across_2, across_1p, across_2p],
        state,
    )
    members = lax.axis_size("branch") * lax.axis_size("tp")
    attended, stats = attend(
        table(pair(y3, core) + pair(y3, other)),
        q,
        start_column,
        [across_3, across_3p],
        state,
        (norm_gain, head_weight),
        members,
    )
    everyone = lax.all_to_all(stats, ("branch", "tp"), 0, 0, tiled=True)
    sums = everyone.reshape(lax.axis_size("branch"), lax.axis_size("tp"), 2, rows).sum(axis=1)
    inverses = lax.rsqrt(sums[:, 0] / D + EPSILON)
    joined = jnp.sum(inverses * sums[:, 1], axis=0)
    inverse = lax.dynamic_index_in_dim(inverses, lax.axis_index("branch"), 0, keepdims=False)
    normed = (attended.astype(jnp.float32) * inverse[:, None] * norm_gain).astype(jnp.bfloat16)
    return (normed[None], joined)


def solution(mesh):
    return jax.shard_map(
        local,
        mesh=mesh,
        in_specs=(
            P("branch", "ctx", "tp"),
            P("branch", "ctx", "tp"),
            P("branch", "ctx", "tp"),
            P(),
            P("branch", "tp"),
            P("branch", "tp"),
        ),
        out_specs=(P("branch", "ctx", "tp"), P("ctx")),
        check_vma=False,
    )
```

```python
import functools
import math

import jax
import jax.numpy as jnp
from jax import lax
from jax.experimental import pallas as pl
from jax.experimental.pallas import tpu as pltpu
from jax.sharding import PartitionSpec as P

HD = 128
D = 8192
NEGATIVE = -1e30
EPSILON = 1e-06

NX, NY = 4, 4
AHEAD, BEHIND = 2, 1


VMEM = pl.BlockSpec(memory_space=pltpu.VMEM)
SMEM = pl.BlockSpec(memory_space=pltpu.SMEM)


def unpack(d):
    return d // (2 * NY), (d // 2) % NY, d % 2


def pack(x, y, core):
    return (x * NY + y) * 2 + core


def moved(block, target):
    route = []
    for d in range(2 * NX * NY):
        x, y, core = target(*unpack(d))
        if 0 <= x < NX and 0 <= y < NY:
            route.append((d, pack(x, y, core)))
    return lax.ppermute(block, "ctx", route)


def attend_kernel(plan, first, last, members, *refs):
    meta, q_ref = refs[:2]
    kv_refs, refs = refs[2 : 2 + len(plan)], refs[2 + len(plan) :]
    if not first:
        m_in, l_in, acc_in = refs[:3]
        refs = refs[3:]
    if last:
        gain_weight = refs[0]
        att_ref, stats_ref, m_ref, l_ref, acc_ref = refs[1:]
    else:
        m_ref, l_ref, acc_ref = refs
    rows = q_ref.shape[0]
    heads = q_ref.shape[1] // HD
    keys = kv_refs[0].shape[2]
    factor = math.log2(math.e) / math.sqrt(HD)

    here = meta[0]
    x, y, core = here // (2 * NY), (here // 2) % NY, here % 2
    first_row = here * rows
    bounds = [meta[i] for i in (1, 2, 3)]

    def start_of(position):
        start = jnp.zeros_like(position)
        for bound in bounds:
            start = jnp.maximum(start, jnp.where(bound <= position, bound, 0))
        return start

    low, high = start_of(first_row), start_of(first_row + rows - 1)

    if first:
        m_ref[...] = jnp.full_like(m_ref, NEGATIVE)
        l_ref[...] = jnp.zeros_like(l_ref)
        acc_ref[...] = jnp.zeros_like(acc_ref)
    else:
        m_ref[...] = m_in[...]
        l_ref[...] = l_in[...]
        acc_ref[...] = acc_in[...]

    def visit(key_rows, value_rows, offset, masked):
        tall = jnp.concatenate([value_rows.T, jnp.ones((16, keys), jnp.bfloat16)], axis=0)
        if masked:
            key_pos = offset + lax.broadcasted_iota(jnp.int32, (keys, rows), 0)
            query_pos = first_row + lax.broadcasted_iota(jnp.int32, (1, rows), 1)
            allowed = (key_pos >= start_of(query_pos)) & (key_pos <= query_pos)

        def scores_of(g):
            return lax.dot_general(
                key_rows,
                q_ref[:, g * HD : (g + 1) * HD],
                (((1,), (1,)), ((), ())),
                preferred_element_type=jnp.float32,
            )

        def mix(g, weights, rescale):
            mixed = jnp.dot(tall, weights, preferred_element_type=jnp.float32)
            l_ref[g] = l_ref[g] * rescale + mixed[HD : HD + 8]
            held = acc_ref[g].reshape(HD // 8, 8, rows) * rescale[None]
            acc_ref[g] = held.reshape(HD, rows) + mixed[:HD]

        ready = {g: scores_of(g) for g in range(min(AHEAD, heads))}
        waiting = []
        for g in range(heads):
            if g + AHEAD < heads:
                ready[g + AHEAD] = scores_of(g + AHEAD)
            scores = ready.pop(g)
            if masked:
                scores = jnp.where(allowed, scores, NEGATIVE)
            scores = scores.reshape(keys // 8, 8, rows)
            old = m_ref[g]
            top = jnp.max(jnp.max(scores, axis=0), axis=0, keepdims=True)
            new = jnp.maximum(old, jnp.broadcast_to(top, old.shape))
            m_ref[g] = new
            rescale = jnp.exp2((old - new) * factor)
            weights = jnp.exp2((scores - new[None]) * factor)
            waiting.append((g, weights.reshape(keys, rows).astype(jnp.bfloat16), rescale))
            if len(waiting) > BEHIND:
                mix(*waiting.pop(0))
        for entry in waiting:
            mix(*entry)

    for kv_ref, (shift, across, flip) in zip(kv_refs, plan):
        count = kv_ref.shape[0]
        yy = jnp.bitwise_xor(y, across)
        base = x + shift if shift is not None else jnp.where(yy < y, x - 1, x - 2)

        def one(i, carry, kv_ref=kv_ref, base=base, yy=yy, flip=flip, own=(shift == 0)):
            j = kv_ref.shape[0] - 1 - i
            xx = base + j
            offset = pack(xx, yy, jnp.bitwise_xor(core, flip)) * rows
            valid = (xx >= 0) & (offset <= first_row) & (offset + keys > low)
            clear = (offset >= high) & (offset + keys <= first_row)

            if not own:

                @pl.when(valid & clear)
                def _():
                    visit(kv_ref[j, 0], kv_ref[j, 1], offset, False)

            @pl.when(valid if own else valid & ~clear)
            def _():
                visit(kv_ref[j, 0], kv_ref[j, 1], offset, True)

            return carry

        lax.fori_loop(0, count, one, 0)

    if last:
        squares = jnp.zeros((8, rows), jnp.float32)
        dotted = jnp.zeros((8, rows), jnp.float32)
        for g in range(heads):
            part = acc_ref[g].reshape(HD // 8, 8, rows) / l_ref[g][None]
            attended = part.reshape(HD, rows).astype(jnp.bfloat16)
            att_ref[g] = attended
            wide = attended.astype(jnp.float32)
            squares += jnp.sum((wide * wide).reshape(HD // 8, 8, rows), axis=0)
            dotted += jnp.sum((wide * gain_weight[g]).reshape(HD // 8, 8, rows), axis=0)
        for n, value in enumerate((squares, dotted)):
            line = jnp.sum(value, axis=0, keepdims=True)
            stats_ref[:, n * rows : (n + 1) * rows] = jnp.broadcast_to(line, (members, rows))


def attend(meta, queries, blocks, plan, state=None, gain_weight=None, members=0):
    rows, width = queries.shape
    heads = width // HD
    first, last = state is None, gain_weight is not None
    shapes = [
        pltpu.VMEM((heads, 8, rows), jnp.float32),
        pltpu.VMEM((heads, 8, rows), jnp.float32),
        pltpu.VMEM((heads, HD, rows), jnp.float32),
    ]
    operands = [meta, queries, *blocks]
    if not first:
        operands += list(state)
    if last:
        operands.append(gain_weight)
        out_shape = (
            jax.ShapeDtypeStruct((heads, HD, rows), jnp.bfloat16),
            jax.ShapeDtypeStruct((members, 2 * rows), jnp.float32),
        )
        scratch = shapes
    else:
        out_shape = tuple(jax.ShapeDtypeStruct(s.shape, s.dtype) for s in shapes)
        scratch = []
    pairs = sum(b.shape[0] for b in blocks) * blocks[0].shape[2] * rows * heads
    return pl.pallas_call(
        functools.partial(attend_kernel, plan, first, last, members),
        out_shape=out_shape,
        in_specs=[SMEM] + [VMEM] * (len(operands) - 1),
        out_specs=(VMEM,) * len(out_shape),
        scratch_shapes=scratch,
        cost_estimate=pl.CostEstimate(
            flops=4 * pairs * HD, bytes_accessed=8 * rows * width, transcendentals=pairs
        ),
        name="attend",
    )(*operands)


def finish_kernel(branches, meta, everyone, att_ref, gain_ref, normed_ref, joined_ref):
    heads, _, rows = att_ref.shape
    sums = everyone[...]
    size = sums.shape[0] // branches
    mine = meta[4]
    joined = jnp.zeros((1, rows), jnp.float32)
    own = jnp.zeros((1, rows), jnp.float32)
    for b in range(branches):
        total = jnp.sum(sums[b * size : (b + 1) * size], axis=0, keepdims=True)
        inverse = lax.rsqrt(total[:, :rows] / D + EPSILON)
        joined += inverse * total[:, rows:]
        own = jnp.where(mine == b, inverse, own)
    joined_ref[...] = joined
    for g in range(heads):
        scaled = att_ref[g].astype(jnp.float32) * own * gain_ref[g]
        normed_ref[:, g * HD : (g + 1) * HD] = scaled.T.astype(jnp.bfloat16)


def finish(meta, everyone, attended, gain, branches):
    heads, _, rows = attended.shape
    return pl.pallas_call(
        functools.partial(finish_kernel, branches),
        out_shape=(
            jax.ShapeDtypeStruct((rows, heads * HD), jnp.bfloat16),
            jax.ShapeDtypeStruct((1, rows), jnp.float32),
        ),
        in_specs=[SMEM] + [VMEM] * 3,
        out_specs=(VMEM,) * 2,
        name="finish",
    )(meta, everyone, attended, gain)


def local(queries, keys, values, segments, norm_gain, head_weight):
    rows = queries.shape[1]
    here = lax.axis_index("ctx")
    y = (here // 2) % NY
    q = queries[0]
    heads = q.shape[1] // HD

    own = jnp.stack([keys[0], values[0]])[None]
    partner = lambda b: moved(b, lambda x, y, c: (x, y, c ^ 1))
    from_1 = moved(own, lambda x, y, c: (x + 1, y, c))
    from_2 = moved(own, lambda x, y, c: (x + 2, y, c))
    own_p = partner(own)

    counts = [jnp.sum(segments < s, dtype=jnp.int32) for s in (1, 2, 3)]
    meta = jnp.stack([here, *counts, lax.axis_index("branch")]).astype(jnp.int32)
    gain_column = norm_gain.reshape(heads, HD, 1)
    weight_column = (norm_gain * head_weight).reshape(heads, HD, 1)

    state = attend(meta, q, [own, own_p], ((0, 0, 0), (0, 0, 1)))
    rising = jnp.concatenate([from_1, own])
    falling = jnp.concatenate([from_2, from_1])
    across_2 = moved(jnp.where(y < 2, rising, falling), lambda x, y, c: (x, y ^ 2, c))
    across_1 = moved(jnp.where(y % 2 == 0, rising, falling), lambda x, y, c: (x, y ^ 1, c))
    falling_p = partner(falling)
    state = attend(meta, q, [falling, falling_p], ((-2, 0, 0), (-2, 0, 1)), state)
    across_2, state = lax.optimization_barrier((across_2, state))
    across_3 = moved(across_2, lambda x, y, c: (x, y ^ 1, c))
    near = jnp.concatenate([across_1, across_2])
    near_p = partner(near)
    state = attend(meta, q, [across_1, across_2], ((None, 1, 0), (None, 2, 0)), state)
    across_3, state = lax.optimization_barrier((across_3, state))
    across_3p = partner(across_3)
    state = attend(
        meta, q, [near_p[:2], near_p[2:]], ((None, 1, 1), (None, 2, 1)), state
    )
    branches = lax.axis_size("branch")
    members = branches * lax.axis_size("tp")
    attended, stats = attend(
        meta,
        q,
        [across_3, across_3p],
        ((None, 3, 0), (None, 3, 1)),
        state,
        weight_column,
        members,
    )
    everyone = lax.all_to_all(stats, ("branch", "tp"), 0, 0, tiled=True)
    normed, joined = finish(meta, everyone, attended, gain_column, branches)
    return (normed[None], joined[0])


def solution(mesh):
    return jax.shard_map(
        local,
        mesh=mesh,
        in_specs=(
            P("branch", "ctx", "tp"),
            P("branch", "ctx", "tp"),
            P("branch", "ctx", "tp"),
            P(),
            P("branch", "tp"),
            P("branch", "tp"),
        ),
        out_specs=(P("branch", "ctx", "tp"), P("ctx")),
        check_vma=False,
    )
```

```python
import functools
import math

import jax
import jax.numpy as jnp
from jax import lax
from jax.experimental import pallas as pl
from jax.experimental.pallas import tpu as pltpu
from jax.sharding import PartitionSpec as P


HD = 128
D = 8192
NEGATIVE = -1e30
EPSILON = 1e-06

NX, NY = 4, 4
AHEAD, BEHIND = 2, 1


VMEM = pl.BlockSpec(memory_space=pltpu.VMEM)
SMEM = pl.BlockSpec(memory_space=pltpu.SMEM)


def unpack(d):
    return d // (2 * NY), (d // 2) % NY, d % 2


def pack(x, y, core):
    return (x * NY + y) * 2 + core


def moved(block, target):
    route = []
    for d in range(2 * NX * NY):
        x, y, core = target(*unpack(d))
        if 0 <= x < NX and 0 <= y < NY:
            route.append((d, pack(x, y, core)))
    return lax.ppermute(block, "ctx", route)


def attend_kernel(plan, first, last, members, *refs):
    if first:
        here_ref, segments_ref, q_ref = refs[:3]
        refs = refs[3:]
    else:
        meta_ref, q_ref = refs[:2]
        refs = refs[2:]
    kv_refs, refs = refs[: len(plan)], refs[len(plan) :]
    if not first:
        m_in, l_in, acc_in = refs[:3]
        refs = refs[3:]
    if last:
        gain_ref, weight_ref = refs[:2]
        att_ref, stats_ref, m_ref, l_ref, acc_ref = refs[2:]
    elif first:
        meta_ref, m_ref, l_ref, acc_ref = refs
    else:
        m_ref, l_ref, acc_ref = refs
    rows = q_ref.shape[0]
    heads = q_ref.shape[1] // HD
    keys = kv_refs[0].shape[2]
    factor = math.log2(math.e) / math.sqrt(HD)

    if first:
        here = here_ref[0]
        segments = segments_ref[...]
        meta_ref[0] = here
        bounds = []
        for s in (1, 2, 3):
            ahead = jnp.sum((segments < s).astype(jnp.float32)).astype(jnp.int32)
            meta_ref[s] = ahead
            bounds.append(ahead)
    else:
        here = meta_ref[0]
        bounds = [meta_ref[s] for s in (1, 2, 3)]
    x, y, core = here >> 3, (here >> 1) & (NY - 1), here & 1
    first_row = here * rows

    def start_of(position):
        start = jnp.zeros_like(position)
        for bound in bounds:
            start = jnp.maximum(start, jnp.where(bound <= position, bound, 0))
        return start

    low, high = start_of(first_row), start_of(first_row + rows - 1)

    if first:
        m_ref[...] = jnp.full_like(m_ref, NEGATIVE)
        l_ref[...] = jnp.zeros_like(l_ref)
        acc_ref[...] = jnp.zeros_like(acc_ref)
    else:
        m_ref[...] = m_in[...]
        l_ref[...] = l_in[...]
        acc_ref[...] = acc_in[...]

    def visit(key_rows, value_rows, offset, masked):
        tall = jnp.concatenate([value_rows.T, jnp.ones((16, keys), jnp.bfloat16)], axis=0)
        if masked:
            key_pos = offset + lax.broadcasted_iota(jnp.int32, (keys, rows), 0)
            query_pos = first_row + lax.broadcasted_iota(jnp.int32, (1, rows), 1)
            allowed = (key_pos >= start_of(query_pos)) & (key_pos <= query_pos)

        def scores_of(g):
            return lax.dot_general(
                key_rows,
                q_ref[:, g * HD : (g + 1) * HD],
                (((1,), (1,)), ((), ())),
                preferred_element_type=jnp.float32,
            )

        def mix(g, weights, rescale):
            mixed = jnp.dot(tall, weights, preferred_element_type=jnp.float32)
            l_ref[g] = l_ref[g] * rescale + mixed[HD : HD + 8]
            held = acc_ref[g].reshape(HD // 8, 8, rows) * rescale[None]
            acc_ref[g] = held.reshape(HD, rows) + mixed[:HD]

        ready = {g: scores_of(g) for g in range(min(AHEAD, heads))}
        waiting = []
        for g in range(heads):
            if g + AHEAD < heads:
                ready[g + AHEAD] = scores_of(g + AHEAD)
            scores = ready.pop(g)
            if masked:
                scores = jnp.where(allowed, scores, NEGATIVE)
            scores = scores.reshape(keys // 8, 8, rows)
            old = m_ref[g]
            top = jnp.max(jnp.max(scores, axis=0), axis=0, keepdims=True)
            new = jnp.maximum(old, jnp.broadcast_to(top, old.shape))
            m_ref[g] = new
            rescale = jnp.exp2((old - new) * factor)
            weights = jnp.exp2((scores - new[None]) * factor)
            waiting.append((g, weights.reshape(keys, rows).astype(jnp.bfloat16), rescale))
            if len(waiting) > BEHIND:
                mix(*waiting.pop(0))
        for entry in waiting:
            mix(*entry)

    for kv_ref, (count, shift, across, flip) in zip(kv_refs, plan):

        def one(i, carry, kv_ref=kv_ref, count=count, shift=shift, across=across, flip=flip):
            j = count - 1 - i
            if shift is not None:
                yy, xx = y, x + shift + j
            else:
                other = across if isinstance(across, int) else jnp.where(j < 2, *across)
                yy = jnp.bitwise_xor(y, other)
                xx = jnp.where(yy < y, x - 1, x - 2) + (j & 1)
            offset = (((xx * NY + yy) * 2) + jnp.bitwise_xor(core, flip)) * rows
            valid = (xx >= 0) & (offset <= first_row) & (offset + keys > low)
            clear = (offset >= high) & (offset + keys <= first_row)

            if not first:

                @pl.when(valid & clear)
                def _():
                    visit(kv_ref[j, 0], kv_ref[j, 1], offset, False)

            @pl.when(valid if first else valid & ~clear)
            def _():
                visit(kv_ref[j, 0], kv_ref[j, 1], offset, True)

            return carry

        lax.fori_loop(0, count, one, 0)

    if last:
        squares = jnp.zeros((8, rows), jnp.float32)
        dotted = jnp.zeros((8, rows), jnp.float32)
        product = gain_ref[...] * weight_ref[...]
        pieces = []
        for _ in range(3):
            pieces.append(product.astype(jnp.bfloat16))
            product = product - pieces[-1].astype(jnp.float32)
        pieces = jnp.concatenate(
            [p.astype(jnp.float32) for p in pieces] + [jnp.zeros((5, product.shape[1]), jnp.float32)],
            axis=0,
        ).astype(jnp.bfloat16)
        for g in range(heads):
            part = acc_ref[g].reshape(HD // 8, 8, rows) / l_ref[g][None]
            attended = part.reshape(HD, rows).astype(jnp.bfloat16)
            att_ref[g] = attended
            wide = attended.astype(jnp.float32)
            squares += jnp.sum((wide * wide).reshape(HD // 8, 8, rows), axis=0)
            dotted += jnp.dot(
                pieces[:, g * HD : (g + 1) * HD], attended, preferred_element_type=jnp.float32
            )
        line = jnp.concatenate(
            [jnp.sum(v, axis=0, keepdims=True) for v in (squares, dotted)], axis=1
        )
        for i in range(members):
            stats_ref[i] = line


SMALL = pltpu.CompilerParams(vmem_limit_bytes=16 * 1024 * 1024)


def attend(operands, blocks, plan, state=None, gains=None, members=0):
    first, last = state is None, gains is not None
    rows, width = operands[-1].shape
    heads = width // HD
    state_shapes = [(heads, 8, rows), (heads, 8, rows), (heads, HD, rows)]
    operands = [*operands, *blocks, *(state or ()), *(gains or ())]
    scratch = []
    if last:
        out_shape = (
            jax.ShapeDtypeStruct((heads, HD, rows), jnp.bfloat16),
            jax.ShapeDtypeStruct((members, 1, 2 * rows), jnp.float32),
        )
        out_specs = (VMEM, VMEM)
        scratch = [pltpu.VMEM(s, jnp.float32) for s in state_shapes]
    else:
        out_shape = tuple(jax.ShapeDtypeStruct(s, jnp.float32) for s in state_shapes)
        out_specs = (VMEM,) * 3
        if first:
            out_shape = (jax.ShapeDtypeStruct((4,), jnp.int32),) + out_shape
            out_specs = (SMEM,) + out_specs
    pairs = sum(p[0] for p in plan) * blocks[0].shape[2] * rows * heads
    return pl.pallas_call(
        functools.partial(attend_kernel, plan, first, last, members),
        out_shape=out_shape,
        in_specs=[SMEM] + [VMEM] * (len(operands) - 1),
        out_specs=out_specs,
        scratch_shapes=scratch,
        compiler_params=SMALL,
        cost_estimate=pl.CostEstimate(
            flops=4 * pairs * HD, bytes_accessed=4 * rows * width, transcendentals=pairs
        ),
        name="attend",
    )(*operands)


def prepare_kernel(att_ref, gain_ref, out_ref):
    heads = att_ref.shape[0]
    for g in range(heads):
        at = slice(g * HD, (g + 1) * HD)
        out_ref[:, at] = att_ref[g].astype(jnp.float32).T * gain_ref[:, at]


def finish_kernel(branches, mine_ref, everyone, scaled_ref, normed_ref, joined_ref):
    rows, width = scaled_ref.shape
    size = everyone.shape[0] // branches
    mine = mine_ref[0]
    joined = jnp.zeros((1, rows), jnp.float32)
    own = jnp.zeros((1, rows), jnp.float32)
    for b in range(branches):
        total = everyone[b * size]
        for i in range(1, size):
            total = total + everyone[b * size + i]
        inverse = lax.rsqrt(total[:, :rows] / D + EPSILON)
        joined += inverse * total[:, rows:]
        own = jnp.where(mine == b, inverse, own)
    joined_ref[...] = joined
    tall = jnp.broadcast_to(own, (HD, rows)).T
    for g in range(width // HD):
        at = slice(g * HD, (g + 1) * HD)
        normed_ref[:, at] = (scaled_ref[:, at] * tall).astype(jnp.bfloat16)


def local(queries, keys, values, segments, norm_gain, head_weight):
    rows = queries.shape[1]
    here = lax.axis_index("ctx")
    y = (here >> 1) & (NY - 1)
    q = queries[0]
    rows, width = q.shape

    own = jnp.stack([keys[0], values[0]])[None]
    partner = lambda b: moved(b, lambda x, y, c: (x, y, c ^ 1))
    from_1 = moved(own, lambda x, y, c: (x + 1, y, c))
    from_2 = moved(own, lambda x, y, c: (x + 2, y, c))

    meta, *state = attend(
        [here.reshape(1), segments.reshape(-1, HD), q], [own], ((1, 0, 0, 0),)
    )
    column = jnp.concatenate([from_2, from_1, own])
    pick = lambda up: jnp.where(up, column[1:], column[:2])
    across_2 = moved(pick(y < 2), lambda x, y, c: (x, y ^ 2, c))
    across_1 = moved(pick((y & 1) == 0), lambda x, y, c: (x, y ^ 1, c))
    column_p = partner(column)
    state = attend([meta, q], [column, column_p], ((2, -2, 0, 0), (3, -2, 0, 1)), state)
    state = attend([meta, q], [across_1], ((2, None, 1, 0),), state)
    across_3 = moved(across_2, lambda x, y, c: (x, y ^ 1, c))
    near = jnp.concatenate([across_1, across_2])
    near_p = partner(near)
    state = attend([meta, q], [across_2], ((2, None, 2, 0),), state)
    state = attend([meta, q], [near_p], ((4, None, (1, 2), 1),), state)
    across_3p = partner(across_3)
    state = attend([meta, q], [across_3], ((2, None, 3, 0),), state)
    branches = lax.axis_size("branch")
    members = branches * lax.axis_size("tp")
    attended, stats = attend(
        [meta, q],
        [across_3p],
        ((2, None, 3, 1),),
        state,
        (norm_gain, head_weight),
        members,
    )
    everyone = lax.all_to_all(stats, ("branch", "tp"), 0, 0, tiled=True)
    scaled = pl.pallas_call(
        prepare_kernel,
        out_shape=jax.ShapeDtypeStruct((rows, width), jnp.float32),
        in_specs=[VMEM] * 2,
        out_specs=VMEM,
        compiler_params=SMALL,
        name="prepare",
    )(attended, norm_gain)
    normed, joined = pl.pallas_call(
        functools.partial(finish_kernel, branches),
        out_shape=(
            jax.ShapeDtypeStruct((rows, width), jnp.bfloat16),
            jax.ShapeDtypeStruct((1, rows), jnp.float32),
        ),
        in_specs=[SMEM] + [VMEM] * 2,
        out_specs=(VMEM,) * 2,
        compiler_params=SMALL,
        name="finish",
    )(lax.axis_index("branch").reshape(1), everyone, scaled)
    return (normed[None], joined[0])


def solution(mesh):
    return jax.shard_map(
        local,
        mesh=mesh,
        in_specs=(
            P("branch", "ctx", "tp"),
            P("branch", "ctx", "tp"),
            P("branch", "ctx", "tp"),
            P(),
            P("branch", "tp"),
            P("branch", "tp"),
        ),
        out_specs=(P("branch", "ctx", "tp"), P("ctx")),
        check_vma=False,
    )
```

```python
import functools
import math

import jax
import jax.numpy as jnp
from jax import lax
from jax.experimental import pallas as pl
from jax.experimental.pallas import tpu as pltpu
from jax.sharding import PartitionSpec as P


HD = 128
D = 8192
NEGATIVE = -1e30
EPSILON = 1e-06

NX, NY = 4, 4
AHEAD, BEHIND = 2, 1


VMEM = pl.BlockSpec(memory_space=pltpu.VMEM)
SMEM = pl.BlockSpec(memory_space=pltpu.SMEM)


def unpack(d):
    return d // (2 * NY), (d // 2) % NY, d % 2


def pack(x, y, core):
    return (x * NY + y) * 2 + core


def moved(block, target):
    route = []
    for d in range(2 * NX * NY):
        x, y, core = target(*unpack(d))
        if 0 <= x < NX and 0 <= y < NY:
            route.append((d, pack(x, y, core)))
    return lax.ppermute(block, "ctx", route)


def attend_kernel(plan, first, last, members, *refs):
    if first:
        here_ref, branch_ref, gain_ref, weight_ref, segments_ref, q_ref = refs[:6]
        refs = refs[6:]
    else:
        meta_ref, q_ref = refs[:2]
        refs = refs[2:]
    kv_refs, refs = refs[: len(plan)], refs[len(plan) :]
    if not first:
        m_in, l_in, acc_in = refs[:3]
        refs = refs[3:]
    if last:
        gain_ref, pieces_ref = refs[:2]
        scaled_ref, stats_ref, m_ref, l_ref, acc_ref = refs[2:]
    elif first:
        meta_ref, held_gain_ref, pieces_ref, m_ref, l_ref, acc_ref = refs
    else:
        m_ref, l_ref, acc_ref = refs
    rows = q_ref.shape[0]
    heads = q_ref.shape[1] // HD
    keys = kv_refs[0].shape[2]
    factor = math.log2(math.e) / math.sqrt(HD)

    if first:
        here = here_ref[0]
        segments = segments_ref[...]
        meta_ref[0] = here
        meta_ref[4] = branch_ref[0]
        gain = gain_ref[...]
        held_gain_ref[...] = gain
        rest = gain * weight_ref[...]
        pieces = []
        for _ in range(3):
            pieces.append(rest.astype(jnp.bfloat16).astype(jnp.float32))
            rest = rest - pieces[-1]
        pieces.append(jnp.zeros((5, rest.shape[1]), jnp.float32))
        pieces_ref[...] = jnp.concatenate(pieces, axis=0).astype(jnp.bfloat16)
        bounds = []
        for s in (1, 2, 3):
            ahead = jnp.sum((segments < s).astype(jnp.float32)).astype(jnp.int32)
            meta_ref[s] = ahead
            bounds.append(ahead)
    else:
        here = meta_ref[0]
        bounds = [meta_ref[s] for s in (1, 2, 3)]
    x, y, core = here >> 3, (here >> 1) & (NY - 1), here & 1
    first_row = here * rows

    def start_of(position):
        start = jnp.zeros_like(position)
        for bound in bounds:
            start = jnp.maximum(start, jnp.where(bound <= position, bound, 0))
        return start

    low, high = start_of(first_row), start_of(first_row + rows - 1)

    if first:
        m_ref[...] = jnp.full_like(m_ref, NEGATIVE)
        l_ref[...] = jnp.zeros_like(l_ref)
        acc_ref[...] = jnp.zeros_like(acc_ref)
    else:
        m_ref[...] = m_in[...]
        l_ref[...] = l_in[...]
        acc_ref[...] = acc_in[...]

    def visit(key_rows, value_rows, offset, masked):
        tall = jnp.concatenate([value_rows.T, jnp.ones((16, keys), jnp.bfloat16)], axis=0)
        if masked:
            key_pos = offset + lax.broadcasted_iota(jnp.int32, (keys, rows), 0)
            query_pos = first_row + lax.broadcasted_iota(jnp.int32, (1, rows), 1)
            allowed = (key_pos >= start_of(query_pos)) & (key_pos <= query_pos)

        def scores_of(g):
            return lax.dot_general(
                key_rows,
                q_ref[:, g * HD : (g + 1) * HD],
                (((1,), (1,)), ((), ())),
                preferred_element_type=jnp.float32,
            )

        def mix(g, weights, rescale):
            mixed = jnp.dot(tall, weights, preferred_element_type=jnp.float32)
            l_ref[g] = l_ref[g] * rescale + mixed[HD : HD + 8]
            held = acc_ref[g].reshape(HD // 8, 8, rows) * rescale[None]
            acc_ref[g] = held.reshape(HD, rows) + mixed[:HD]

        ready = {g: scores_of(g) for g in range(min(AHEAD, heads))}
        waiting = []
        for g in range(heads):
            if g + AHEAD < heads:
                ready[g + AHEAD] = scores_of(g + AHEAD)
            scores = ready.pop(g)
            if masked:
                scores = jnp.where(allowed, scores, NEGATIVE)
            scores = scores.reshape(keys // 8, 8, rows)
            old = m_ref[g]
            top = jnp.max(jnp.max(scores, axis=0), axis=0, keepdims=True)
            new = jnp.maximum(old, jnp.broadcast_to(top, old.shape))
            m_ref[g] = new
            rescale = jnp.exp2((old - new) * factor)
            weights = jnp.exp2((scores - new[None]) * factor)
            waiting.append((g, weights.reshape(keys, rows).astype(jnp.bfloat16), rescale))
            if len(waiting) > BEHIND:
                mix(*waiting.pop(0))
        for entry in waiting:
            mix(*entry)

    for kv_ref, (count, shift, across, flip) in zip(kv_refs, plan):

        def one(i, carry, kv_ref=kv_ref, count=count, shift=shift, across=across, flip=flip):
            j = count - 1 - i
            if shift is not None:
                yy, xx = y, x + shift + j
            else:
                other = across if isinstance(across, int) else jnp.where(j < 2, *across)
                yy = jnp.bitwise_xor(y, other)
                xx = jnp.where(yy < y, x - 1, x - 2) + (j & 1)
            offset = (((xx * NY + yy) * 2) + jnp.bitwise_xor(core, flip)) * rows
            valid = (xx >= 0) & (offset <= first_row) & (offset + keys > low)
            clear = (offset >= high) & (offset + keys <= first_row)

            if not first:

                @pl.when(valid & clear)
                def _():
                    visit(kv_ref[j, 0], kv_ref[j, 1], offset, False)

            @pl.when(valid if first else valid & ~clear)
            def _():
                visit(kv_ref[j, 0], kv_ref[j, 1], offset, True)

            return carry

        lax.fori_loop(0, count, one, 0)

    if last:
        squares = jnp.zeros((8, rows), jnp.float32)
        dotted = jnp.zeros((8, rows), jnp.float32)
        for g in range(heads):
            part = acc_ref[g].reshape(HD // 8, 8, rows) / l_ref[g][None]
            attended = part.reshape(HD, rows).astype(jnp.bfloat16)
            wide = attended.astype(jnp.float32)
            at = slice(g * HD, (g + 1) * HD)
            scaled_ref[:, at] = wide.T * gain_ref[:, at]
            squares += jnp.sum((wide * wide).reshape(HD // 8, 8, rows), axis=0)
            dotted += jnp.dot(
                pieces_ref[:, at], attended, preferred_element_type=jnp.float32
            )
        line = jnp.concatenate(
            [jnp.sum(v, axis=0, keepdims=True) for v in (squares, dotted)], axis=1
        )
        for i in range(members):
            stats_ref[i] = line


SMALL = pltpu.CompilerParams(vmem_limit_bytes=16 * 1024 * 1024)


def attend(operands, blocks, plan, state=None, gains=None, members=0):
    first, last = state is None, gains is not None
    rows, width = operands[-1].shape
    heads = width // HD
    state_shapes = [(heads, 8, rows), (heads, 8, rows), (heads, HD, rows)]
    operands = [*operands, *blocks, *(state or ()), *(gains or ())]
    scratch = []
    scalars = 2 if first else 1
    if last:
        out_shape = (
            jax.ShapeDtypeStruct((rows, width), jnp.float32),
            jax.ShapeDtypeStruct((members, 1, 2 * rows), jnp.float32),
        )
        out_specs = (VMEM, VMEM)
        scratch = [pltpu.VMEM(s, jnp.float32) for s in state_shapes]
    else:
        out_shape = tuple(jax.ShapeDtypeStruct(s, jnp.float32) for s in state_shapes)
        out_specs = (VMEM,) * 3
        if first:
            out_shape = (
                jax.ShapeDtypeStruct((5,), jnp.int32),
                jax.ShapeDtypeStruct((1, width), jnp.float32),
                jax.ShapeDtypeStruct((8, width), jnp.bfloat16),
            ) + out_shape
            out_specs = (SMEM, VMEM, VMEM) + out_specs
    pairs = sum(p[0] for p in plan) * blocks[0].shape[2] * rows * heads
    return pl.pallas_call(
        functools.partial(attend_kernel, plan, first, last, members),
        out_shape=out_shape,
        in_specs=[SMEM] * scalars + [VMEM] * (len(operands) - scalars),
        out_specs=out_specs,
        scratch_shapes=scratch,
        compiler_params=SMALL,
        cost_estimate=pl.CostEstimate(
            flops=4 * pairs * HD, bytes_accessed=4 * rows * width, transcendentals=pairs
        ),
        name="attend",
    )(*operands)


def finish_kernel(branches, meta_ref, everyone, scaled_ref, normed_ref, joined_ref):
    rows, width = scaled_ref.shape
    size = everyone.shape[0] // branches
    mine = meta_ref[4]
    joined = jnp.zeros((1, rows), jnp.float32)
    own = jnp.zeros((1, rows), jnp.float32)
    for b in range(branches):
        total = everyone[b * size]
        for i in range(1, size):
            total = total + everyone[b * size + i]
        inverse = lax.rsqrt(total[:, :rows] / D + EPSILON)
        joined += inverse * total[:, rows:]
        own = jnp.where(mine == b, inverse, own)
    joined_ref[...] = joined
    tall = jnp.broadcast_to(own, (HD, rows)).T
    for g in range(width // HD):
        at = slice(g * HD, (g + 1) * HD)
        normed_ref[:, at] = (scaled_ref[:, at] * tall).astype(jnp.bfloat16)


def local(queries, keys, values, segments, norm_gain, head_weight):
    rows = queries.shape[1]
    here = lax.axis_index("ctx")
    y = (here >> 1) & (NY - 1)
    q = queries[0]
    rows, width = q.shape

    own = jnp.stack([keys[0], values[0]])[None]
    partner = lambda b: moved(b, lambda x, y, c: (x, y, c ^ 1))
    from_1 = moved(own, lambda x, y, c: (x + 1, y, c))
    from_2 = moved(own, lambda x, y, c: (x + 2, y, c))

    meta, gain, pieces, *state = attend(
        [
            here.reshape(1),
            lax.axis_index("branch").reshape(1),
            norm_gain,
            head_weight,
            segments.reshape(-1, HD),
            q,
        ],
        [own],
        ((1, 0, 0, 0),),
    )
    column = jnp.concatenate([from_2, from_1, own])
    pick = lambda up: jnp.where(up, column[1:], column[:2])
    across_2 = moved(pick(y < 2), lambda x, y, c: (x, y ^ 2, c))
    across_1 = moved(pick((y & 1) == 0), lambda x, y, c: (x, y ^ 1, c))
    column_p = partner(column)
    state = attend([meta, q], [column, column_p], ((2, -2, 0, 0), (3, -2, 0, 1)), state)
    state = attend([meta, q], [across_1], ((2, None, 1, 0),), state)
    across_3 = moved(across_2, lambda x, y, c: (x, y ^ 1, c))
    near = jnp.concatenate([across_1, across_2])
    near_p = partner(near)
    state = attend([meta, q], [across_2], ((2, None, 2, 0),), state)
    state = attend([meta, q], [near_p], ((4, None, (1, 2), 1),), state)
    across_3p = partner(across_3)
    state = attend([meta, q], [across_3], ((2, None, 3, 0),), state)
    branches = lax.axis_size("branch")
    members = branches * lax.axis_size("tp")
    scaled, stats = attend(
        [meta, q], [across_3p], ((2, None, 3, 1),), state, (gain, pieces), members
    )
    everyone = lax.all_to_all(stats, ("branch", "tp"), 0, 0, tiled=True)
    normed, joined = pl.pallas_call(
        functools.partial(finish_kernel, branches),
        out_shape=(
            jax.ShapeDtypeStruct((rows, width), jnp.bfloat16),
            jax.ShapeDtypeStruct((1, rows), jnp.float32),
        ),
        in_specs=[SMEM] + [VMEM] * 2,
        out_specs=(VMEM,) * 2,
        compiler_params=SMALL,
        name="finish",
    )(meta, everyone, scaled)
    return (normed[None], joined[0])


def solution(mesh):
    return jax.shard_map(
        local,
        mesh=mesh,
        in_specs=(
            P("branch", "ctx", "tp"),
            P("branch", "ctx", "tp"),
            P("branch", "ctx", "tp"),
            P(),
            P("branch", "tp"),
            P("branch", "tp"),
        ),
        out_specs=(P("branch", "ctx", "tp"), P("ctx")),
        check_vma=False,
    )
```

```python
import functools
import math

import jax
import jax.numpy as jnp
from jax import lax
from jax.experimental import pallas as pl
from jax.experimental.pallas import tpu as pltpu
from jax.sharding import PartitionSpec as P


HD = 128
D = 8192
NEGATIVE = -1e30
EPSILON = 1e-06

NX, NY = 4, 4
AHEAD, BEHIND = 3, 2


VMEM = pl.BlockSpec(memory_space=pltpu.VMEM)
SMEM = pl.BlockSpec(memory_space=pltpu.SMEM)


def unpack(d):
    return d // (2 * NY), (d // 2) % NY, d % 2


def pack(x, y, core):
    return (x * NY + y) * 2 + core


def moved(block, target):
    route = []
    for d in range(2 * NX * NY):
        x, y, core = target(*unpack(d))
        if 0 <= x < NX and 0 <= y < NY:
            route.append((d, pack(x, y, core)))
    return lax.ppermute(block, "ctx", route)


def attend_kernel(plan, first, last, members, *refs):
    if first:
        here_ref, branch_ref, gain_ref, weight_ref, segments_ref, q_ref = refs[:6]
        refs = refs[6:]
    else:
        meta_ref, q_ref = refs[:2]
        refs = refs[2:]
    kv_refs, refs = refs[: len(plan)], refs[len(plan) :]
    if not first:
        m_in, l_in, acc_in = refs[:3]
        refs = refs[3:]
    if last:
        gain_ref, pieces_ref = refs[:2]
        scaled_ref, stats_ref, m_ref, l_ref, acc_ref = refs[2:]
    elif first:
        meta_ref, side_ref, held_gain_ref, pieces_ref, m_ref, l_ref, acc_ref = refs
    else:
        m_ref, l_ref, acc_ref = refs
    rows = q_ref.shape[0]
    heads = q_ref.shape[1] // HD
    keys = kv_refs[0].shape[2]
    factor = math.log2(math.e) / math.sqrt(HD)

    if first:
        here = here_ref[0]
        segments = segments_ref[...]
        meta_ref[0] = here
        side_ref[...] = jnp.full(side_ref.shape, branch_ref[0], jnp.int32)
        gain = gain_ref[...]
        held_gain_ref[...] = gain
        rest = gain * weight_ref[...]
        pieces = []
        for _ in range(3):
            pieces.append(rest.astype(jnp.bfloat16).astype(jnp.float32))
            rest = rest - pieces[-1]
        pieces.append(jnp.zeros((5, rest.shape[1]), jnp.float32))
        pieces_ref[...] = jnp.concatenate(pieces, axis=0).astype(jnp.bfloat16)
        bounds = []
        for s in (1, 2, 3):
            ahead = jnp.sum((segments < s).astype(jnp.float32)).astype(jnp.int32)
            meta_ref[s] = ahead
            bounds.append(ahead)
    else:
        here = meta_ref[0]
        bounds = [meta_ref[s] for s in (1, 2, 3)]
    x, y, core = here >> 3, (here >> 1) & (NY - 1), here & 1
    first_row = here * rows

    def start_of(position):
        start = jnp.zeros_like(position)
        for bound in bounds:
            start = jnp.maximum(start, jnp.where(bound <= position, bound, 0))
        return start

    low, high = start_of(first_row), start_of(first_row + rows - 1)

    if first:
        m_ref[...] = jnp.full_like(m_ref, NEGATIVE)
        l_ref[...] = jnp.zeros_like(l_ref)
        acc_ref[...] = jnp.zeros_like(acc_ref)
    else:
        m_ref[...] = m_in[...]
        l_ref[...] = l_in[...]
        acc_ref[...] = acc_in[...]

    def visit(kv_ref, entries, offsets, masked):
        join = lambda n: jnp.concatenate([kv_ref[j, n] for j in entries], axis=0)
        key_rows, value_rows = join(0), join(1)
        keys = key_rows.shape[0]
        tall = jnp.concatenate([value_rows.T, jnp.ones((16, keys), jnp.bfloat16)], axis=0)
        if masked:
            within = lax.broadcasted_iota(jnp.int32, (rows, rows), 0)
            key_pos = jnp.concatenate([offset + within for offset in offsets], axis=0)
            query_pos = first_row + lax.broadcasted_iota(jnp.int32, (1, rows), 1)
            allowed = (key_pos >= start_of(query_pos)) & (key_pos <= query_pos)

        def scores_of(g):
            return lax.dot_general(
                key_rows,
                q_ref[:, g * HD : (g + 1) * HD],
                (((1,), (1,)), ((), ())),
                preferred_element_type=jnp.float32,
            )

        def mix(g, weights, rescale):
            mixed = jnp.dot(tall, weights, preferred_element_type=jnp.float32)
            l_ref[g] = l_ref[g] * rescale + mixed[HD : HD + 8]
            held = acc_ref[g].reshape(HD // 8, 8, rows) * rescale[None]
            acc_ref[g] = held.reshape(HD, rows) + mixed[:HD]

        ready = {g: scores_of(g) for g in range(min(AHEAD, heads))}
        waiting = []
        for g in range(heads):
            if g + AHEAD < heads:
                ready[g + AHEAD] = scores_of(g + AHEAD)
            scores = ready.pop(g)
            if masked:
                scores = jnp.where(allowed, scores, NEGATIVE)
            scores = scores.reshape(keys // 8, 8, rows)
            old = m_ref[g]
            top = jnp.max(jnp.max(scores, axis=0), axis=0, keepdims=True)
            new = jnp.maximum(old, jnp.broadcast_to(top, old.shape))
            m_ref[g] = new
            rescale = jnp.exp2((old - new) * factor)
            weights = jnp.exp2((scores - new[None]) * factor)
            waiting.append((g, weights.reshape(keys, rows).astype(jnp.bfloat16), rescale))
            if len(waiting) > BEHIND:
                mix(*waiting.pop(0))
        for entry in waiting:
            mix(*entry)

    for kv_ref, (count, shift, across, flip) in zip(kv_refs, plan):

        def place(j, shift=shift, across=across, flip=flip):
            if shift is not None:
                yy, xx = y, x + shift + j
            else:
                other = across if isinstance(across, int) else jnp.where(j < 2, *across)
                yy = jnp.bitwise_xor(y, other)
                xx = jnp.where(yy < y, x - 1, x - 2) + (j & 1)
            offset = (((xx * NY + yy) * 2) + jnp.bitwise_xor(core, flip)) * rows
            valid = (xx >= 0) & (offset <= first_row) & (offset + keys > low)
            clear = (offset >= high) & (offset + keys <= first_row)
            return offset, valid, clear

        def take(entries, kv_ref=kv_ref, place=place):
            offsets, valids, clears = zip(*[place(j) for j in entries])
            valid, clear = valids[0], valids[0] & clears[0]
            for v, c in zip(valids[1:], clears[1:]):
                valid, clear = valid | v, clear & v & c

            if not first:

                @pl.when(clear)
                def _():
                    visit(kv_ref, entries, offsets, False)

            @pl.when(valid & ~clear)
            def _():
                visit(kv_ref, entries, offsets, True)

        if count == 2:
            take([0, 1])
        elif count > 1:

            def pair(i, carry, take=take):
                take([2 * i, 2 * i + 1])
                return carry

            lax.fori_loop(0, count // 2, pair, 0)
        if count % 2:
            take([count - 1])

    if last:
        squares = jnp.zeros((8, rows), jnp.float32)
        dotted = jnp.zeros((8, rows), jnp.float32)
        for g in range(heads):
            part = acc_ref[g].reshape(HD // 8, 8, rows) / l_ref[g][None]
            attended = part.reshape(HD, rows).astype(jnp.bfloat16)
            wide = attended.astype(jnp.float32)
            at = slice(g * HD, (g + 1) * HD)
            scaled_ref[:, at] = wide.T * gain_ref[:, at]
            squares += jnp.sum((wide * wide).reshape(HD // 8, 8, rows), axis=0)
            dotted += jnp.dot(
                pieces_ref[:, at], attended, preferred_element_type=jnp.float32
            )
        line = jnp.concatenate(
            [jnp.sum(v, axis=0, keepdims=True) for v in (squares, dotted)], axis=1
        )
        for i in range(members):
            stats_ref[i] = line


SMALL = pltpu.CompilerParams(vmem_limit_bytes=16 * 1024 * 1024)


def attend(operands, blocks, plan, state=None, gains=None, members=0):
    first, last = state is None, gains is not None
    rows, width = operands[-1].shape
    heads = width // HD
    state_shapes = [(heads, 8, rows), (heads, 8, rows), (heads, HD, rows)]
    operands = [*operands, *blocks, *(state or ()), *(gains or ())]
    scratch = []
    scalars = 2 if first else 1
    if last:
        out_shape = (
            jax.ShapeDtypeStruct((rows, width), jnp.float32),
            jax.ShapeDtypeStruct((members, 1, 2 * rows), jnp.float32),
        )
        out_specs = (VMEM, VMEM)
        scratch = [pltpu.VMEM(s, jnp.float32) for s in state_shapes]
    else:
        out_shape = tuple(jax.ShapeDtypeStruct(s, jnp.float32) for s in state_shapes)
        out_specs = (VMEM,) * 3
        if first:
            out_shape = (
                jax.ShapeDtypeStruct((4,), jnp.int32),
                jax.ShapeDtypeStruct((1, rows), jnp.int32),
                jax.ShapeDtypeStruct((1, width), jnp.float32),
                jax.ShapeDtypeStruct((8, width), jnp.bfloat16),
            ) + out_shape
            out_specs = (SMEM, VMEM, VMEM, VMEM) + out_specs
    pairs = sum(p[0] for p in plan) * blocks[0].shape[2] * rows * heads
    return pl.pallas_call(
        functools.partial(attend_kernel, plan, first, last, members),
        out_shape=out_shape,
        in_specs=[SMEM] * scalars + [VMEM] * (len(operands) - scalars),
        out_specs=out_specs,
        scratch_shapes=scratch,
        compiler_params=SMALL,
        cost_estimate=pl.CostEstimate(
            flops=4 * pairs * HD, bytes_accessed=4 * rows * width, transcendentals=pairs
        ),
        name="attend",
    )(*operands)


def finish_kernel(branches, side_ref, everyone, scaled_ref, normed_ref, joined_ref):
    rows, width = scaled_ref.shape
    size = everyone.shape[0] // branches
    mine = side_ref[...]
    joined = jnp.zeros((1, rows), jnp.float32)
    own = jnp.zeros((1, rows), jnp.float32)
    for b in range(branches):
        total = everyone[b * size]
        for i in range(1, size):
            total = total + everyone[b * size + i]
        inverse = lax.rsqrt(total[:, :rows] / D + EPSILON)
        joined += inverse * total[:, rows:]
        own = jnp.where(mine == b, inverse, own)
    joined_ref[...] = joined
    tall = jnp.broadcast_to(own, (HD, rows)).T
    for g in range(width // HD):
        at = slice(g * HD, (g + 1) * HD)
        normed_ref[:, at] = (scaled_ref[:, at] * tall).astype(jnp.bfloat16)


def local(queries, keys, values, segments, norm_gain, head_weight):
    rows = queries.shape[1]
    here = lax.axis_index("ctx")
    y = (here >> 1) & (NY - 1)
    q = queries[0]
    rows, width = q.shape

    own = jnp.stack([keys[0], values[0]])[None]
    partner = lambda b: moved(b, lambda x, y, c: (x, y, c ^ 1))
    from_1 = moved(own, lambda x, y, c: (x + 1, y, c))
    from_2 = moved(own, lambda x, y, c: (x + 2, y, c))

    meta, side, gain, pieces, *state = attend(
        [
            here.reshape(1),
            lax.axis_index("branch").reshape(1),
            norm_gain,
            head_weight,
            segments.reshape(-1, HD),
            q,
        ],
        [own],
        ((1, 0, 0, 0),),
    )
    column = jnp.concatenate([from_2, from_1, own])
    pick = lambda up: jnp.where(up, column[1:], column[:2])
    across_2 = moved(pick(y < 2), lambda x, y, c: (x, y ^ 2, c))
    across_1 = moved(pick((y & 1) == 0), lambda x, y, c: (x, y ^ 1, c))
    column_p = partner(column)
    state = attend([meta, q], [column, column_p], ((2, -2, 0, 0), (3, -2, 0, 1)), state)
    state = attend([meta, q], [across_1], ((2, None, 1, 0),), state)
    across_3 = moved(across_2, lambda x, y, c: (x, y ^ 1, c))
    near = jnp.concatenate([across_1, across_2])
    near_p = partner(near)
    state = attend([meta, q], [across_2], ((2, None, 2, 0),), state)
    state = attend([meta, q], [near_p], ((4, None, (1, 2), 1),), state)
    across_3p = partner(across_3)
    state = attend([meta, q], [across_3], ((2, None, 3, 0),), state)
    branches = lax.axis_size("branch")
    members = branches * lax.axis_size("tp")
    scaled, stats = attend(
        [meta, q], [across_3p], ((2, None, 3, 1),), state, (gain, pieces), members
    )
    everyone = lax.all_to_all(stats, ("branch", "tp"), 0, 0, tiled=True)
    normed, joined = pl.pallas_call(
        functools.partial(finish_kernel, branches),
        out_shape=(
            jax.ShapeDtypeStruct((rows, width), jnp.bfloat16),
            jax.ShapeDtypeStruct((1, rows), jnp.float32),
        ),
        in_specs=[VMEM] * 3,
        out_specs=(VMEM,) * 2,
        compiler_params=SMALL,
        name="finish",
    )(side, everyone, scaled)
    return (normed[None], joined[0])


def solution(mesh):
    return jax.shard_map(
        local,
        mesh=mesh,
        in_specs=(
            P("branch", "ctx", "tp"),
            P("branch", "ctx", "tp"),
            P("branch", "ctx", "tp"),
            P(),
            P("branch", "tp"),
            P("branch", "tp"),
        ),
        out_specs=(P("branch", "ctx", "tp"), P("ctx")),
        check_vma=False,
    )
```

```python
import functools
import math

import jax
import jax.numpy as jnp
from jax import lax
from jax.experimental import pallas as pl
from jax.experimental.pallas import tpu as pltpu
from jax.sharding import PartitionSpec as P


HD = 128
D = 8192
NEGATIVE = -1e30
EPSILON = 1e-06

NX, NY = 4, 4
AHEAD, BEHIND = 3, 2


VMEM = pl.BlockSpec(memory_space=pltpu.VMEM)
SMEM = pl.BlockSpec(memory_space=pltpu.SMEM)


def unpack(d):
    return d // (2 * NY), (d // 2) % NY, d % 2


def pack(x, y, core):
    return (x * NY + y) * 2 + core


def moved(block, target):
    route = []
    for d in range(2 * NX * NY):
        x, y, core = target(*unpack(d))
        if 0 <= x < NX and 0 <= y < NY:
            route.append((d, pack(x, y, core)))
    return lax.ppermute(block, "ctx", route)


def attend_kernel(plan, first, last, members, *refs):
    if first:
        here_ref, branch_ref, gain_ref, weight_ref, segments_ref, q_ref = refs[:6]
        refs = refs[6:]
    else:
        meta_ref, q_ref = refs[:2]
        refs = refs[2:]
    kv_refs, refs = refs[: len(plan)], refs[len(plan) :]
    if not first:
        m_in, l_in, acc_in = refs[:3]
        refs = refs[3:]
    if last:
        gain_ref, pieces_ref = refs[:2]
        scaled_ref, stats_ref, m_ref, l_ref, acc_ref = refs[2:]
    elif first:
        meta_ref, parts_ref, side_ref, held_gain_ref, pieces_ref, m_ref, l_ref, acc_ref = refs
    else:
        m_ref, l_ref, acc_ref = refs
    rows = q_ref.shape[0]
    heads = q_ref.shape[1] // (HD if first else 2 * HD)
    keys = kv_refs[0].shape[2]
    factor = math.log2(math.e) / math.sqrt(HD)

    if first:
        for g in range(heads):
            scaled = q_ref[:, g * HD : (g + 1) * HD].astype(jnp.float32) * factor
            high_part = scaled.astype(jnp.bfloat16)
            low_part = (scaled - high_part.astype(jnp.float32)).astype(jnp.bfloat16)
            parts_ref[:, 2 * g * HD : (2 * g + 1) * HD] = high_part
            parts_ref[:, (2 * g + 1) * HD : 2 * (g + 1) * HD] = low_part
        q_ref = parts_ref
        here = here_ref[0]
        segments = segments_ref[...]
        meta_ref[0] = here
        side_ref[...] = jnp.full(side_ref.shape, branch_ref[0], jnp.int32)
        gain = gain_ref[...]
        held_gain_ref[...] = gain
        rest = gain * weight_ref[...]
        pieces = []
        for _ in range(3):
            pieces.append(rest.astype(jnp.bfloat16).astype(jnp.float32))
            rest = rest - pieces[-1]
        pieces.append(jnp.zeros((5, rest.shape[1]), jnp.float32))
        pieces_ref[...] = jnp.concatenate(pieces, axis=0).astype(jnp.bfloat16)
        bounds = []
        for s in (1, 2, 3):
            ahead = jnp.sum((segments < s).astype(jnp.float32)).astype(jnp.int32)
            meta_ref[s] = ahead
            bounds.append(ahead)
    else:
        here = meta_ref[0]
        bounds = [meta_ref[s] for s in (1, 2, 3)]
    x, y, core = here >> 3, (here >> 1) & (NY - 1), here & 1
    first_row = here * rows

    def start_of(position):
        start = jnp.zeros_like(position)
        for bound in bounds:
            start = jnp.maximum(start, jnp.where(bound <= position, bound, 0))
        return start

    low, high = start_of(first_row), start_of(first_row + rows - 1)

    if first:
        m_ref[...] = jnp.full_like(m_ref, NEGATIVE)
        l_ref[...] = jnp.zeros_like(l_ref)
        acc_ref[...] = jnp.zeros_like(acc_ref)
    else:
        m_ref[...] = m_in[...]
        l_ref[...] = l_in[...]
        acc_ref[...] = acc_in[...]

    def visit(kv_ref, entries, offsets, masked):
        join = lambda n: jnp.concatenate([kv_ref[j, n] for j in entries], axis=0)
        key_rows, value_rows = join(0), join(1)
        keys = key_rows.shape[0]
        key_twice = jnp.concatenate([key_rows, key_rows], axis=1)
        tall = jnp.concatenate([value_rows.T, jnp.ones((16, keys), jnp.bfloat16)], axis=0)
        if masked:
            within = lax.broadcasted_iota(jnp.int32, (rows, rows), 0)
            key_pos = jnp.concatenate([offset + within for offset in offsets], axis=0)
            query_pos = first_row + lax.broadcasted_iota(jnp.int32, (1, rows), 1)
            allowed = (key_pos >= start_of(query_pos)) & (key_pos <= query_pos)

        def scores_of(g):
            return lax.dot_general(
                key_twice,
                q_ref[:, 2 * g * HD : 2 * (g + 1) * HD],
                (((1,), (1,)), ((), ())),
                preferred_element_type=jnp.float32,
            )

        def mix(g, weights, rescale):
            mixed = jnp.dot(tall, weights, preferred_element_type=jnp.float32)
            l_ref[g] = l_ref[g] * rescale + mixed[HD : HD + 8]
            held = acc_ref[g].reshape(HD // 8, 8, rows) * rescale[None]
            acc_ref[g] = held.reshape(HD, rows) + mixed[:HD]

        ready = {g: scores_of(g) for g in range(min(AHEAD, heads))}
        waiting = []
        for g in range(heads):
            if g + AHEAD < heads:
                ready[g + AHEAD] = scores_of(g + AHEAD)
            scores = ready.pop(g)
            if masked:
                scores = jnp.where(allowed, scores, NEGATIVE)
            scores = scores.reshape(keys // 8, 8, rows)
            old = m_ref[g]
            top = jnp.max(jnp.max(scores, axis=0), axis=0, keepdims=True)
            new = jnp.maximum(old, jnp.broadcast_to(top, old.shape))
            m_ref[g] = new
            rescale = jnp.exp2(old - new)
            weights = jnp.exp2(scores - new[None])
            waiting.append((g, weights.reshape(keys, rows).astype(jnp.bfloat16), rescale))
            if len(waiting) > BEHIND:
                mix(*waiting.pop(0))
        for entry in waiting:
            mix(*entry)

    for kv_ref, (count, shift, across, flip) in zip(kv_refs, plan):

        def place(j, shift=shift, across=across, flip=flip):
            if shift is not None:
                yy, xx = y, x + shift + j
            else:
                other = across if isinstance(across, int) else jnp.where(j < 2, *across)
                yy = jnp.bitwise_xor(y, other)
                xx = jnp.where(yy < y, x - 1, x - 2) + (j & 1)
            offset = (((xx * NY + yy) * 2) + jnp.bitwise_xor(core, flip)) * rows
            valid = (xx >= 0) & (offset <= first_row) & (offset + keys > low)
            clear = (offset >= high) & (offset + keys <= first_row)
            return offset, valid, clear

        def take(entries, kv_ref=kv_ref, place=place):
            offsets, valids, clears = zip(*[place(j) for j in entries])
            valid, clear = valids[0], valids[0] & clears[0]
            for v, c in zip(valids[1:], clears[1:]):
                valid, clear = valid | v, clear & v & c

            if not first:

                @pl.when(clear)
                def _():
                    visit(kv_ref, entries, offsets, False)

            @pl.when(valid & ~clear)
            def _():
                visit(kv_ref, entries, offsets, True)

        if count == 2:
            take([0, 1])
        elif count > 1:

            def pair(i, carry, take=take):
                take([2 * i, 2 * i + 1])
                return carry

            lax.fori_loop(0, count // 2, pair, 0)
        if count % 2:
            take([count - 1])

    if last:
        squares = jnp.zeros((8, rows), jnp.float32)
        dotted = jnp.zeros((8, rows), jnp.float32)
        for g in range(heads):
            part = acc_ref[g].reshape(HD // 8, 8, rows) / l_ref[g][None]
            attended = part.reshape(HD, rows).astype(jnp.bfloat16)
            wide = attended.astype(jnp.float32)
            at = slice(g * HD, (g + 1) * HD)
            scaled_ref[:, at] = wide.T * gain_ref[:, at]
            squares += jnp.sum((wide * wide).reshape(HD // 8, 8, rows), axis=0)
            dotted += jnp.dot(
                pieces_ref[:, at], attended, preferred_element_type=jnp.float32
            )
        line = jnp.concatenate(
            [jnp.sum(v, axis=0, keepdims=True) for v in (squares, dotted)], axis=1
        )
        for i in range(members):
            stats_ref[i] = line


SMALL = pltpu.CompilerParams(vmem_limit_bytes=16 * 1024 * 1024)


def attend(operands, blocks, plan, state=None, gains=None, members=0):
    first, last = state is None, gains is not None
    rows = operands[-1].shape[0]
    heads = operands[-1].shape[1] // (HD if first else 2 * HD)
    width = heads * HD
    state_shapes = [(heads, 8, rows), (heads, 8, rows), (heads, HD, rows)]
    operands = [*operands, *blocks, *(state or ()), *(gains or ())]
    scratch = []
    scalars = 2 if first else 1
    if last:
        out_shape = (
            jax.ShapeDtypeStruct((rows, width), jnp.float32),
            jax.ShapeDtypeStruct((members, 1, 2 * rows), jnp.float32),
        )
        out_specs = (VMEM, VMEM)
        scratch = [pltpu.VMEM(s, jnp.float32) for s in state_shapes]
    else:
        out_shape = tuple(jax.ShapeDtypeStruct(s, jnp.float32) for s in state_shapes)
        out_specs = (VMEM,) * 3
        if first:
            out_shape = (
                jax.ShapeDtypeStruct((4,), jnp.int32),
                jax.ShapeDtypeStruct((rows, 2 * width), jnp.bfloat16),
                jax.ShapeDtypeStruct((1, rows), jnp.int32),
                jax.ShapeDtypeStruct((1, width), jnp.float32),
                jax.ShapeDtypeStruct((8, width), jnp.bfloat16),
            ) + out_shape
            out_specs = (SMEM, VMEM, VMEM, VMEM, VMEM) + out_specs
    pairs = sum(p[0] for p in plan) * blocks[0].shape[2] * rows * heads
    return pl.pallas_call(
        functools.partial(attend_kernel, plan, first, last, members),
        out_shape=out_shape,
        in_specs=[SMEM] * scalars + [VMEM] * (len(operands) - scalars),
        out_specs=out_specs,
        scratch_shapes=scratch,
        compiler_params=SMALL,
        cost_estimate=pl.CostEstimate(
            flops=4 * pairs * HD, bytes_accessed=4 * rows * width, transcendentals=pairs
        ),
        name="attend",
    )(*operands)


def finish_kernel(branches, side_ref, everyone, scaled_ref, normed_ref, joined_ref):
    rows, width = scaled_ref.shape
    size = everyone.shape[0] // branches
    mine = side_ref[...]
    joined = jnp.zeros((1, rows), jnp.float32)
    own = jnp.zeros((1, rows), jnp.float32)
    for b in range(branches):
        total = everyone[b * size]
        for i in range(1, size):
            total = total + everyone[b * size + i]
        inverse = lax.rsqrt(total[:, :rows] / D + EPSILON)
        joined += inverse * total[:, rows:]
        own = jnp.where(mine == b, inverse, own)
    joined_ref[...] = joined
    tall = jnp.broadcast_to(own, (HD, rows)).T
    for g in range(width // HD):
        at = slice(g * HD, (g + 1) * HD)
        normed_ref[:, at] = (scaled_ref[:, at] * tall).astype(jnp.bfloat16)


def local(queries, keys, values, segments, norm_gain, head_weight):
    rows = queries.shape[1]
    here = lax.axis_index("ctx")
    y = (here >> 1) & (NY - 1)
    q = queries[0]
    rows, width = q.shape

    own = jnp.stack([keys[0], values[0]])[None]
    partner = lambda b: moved(b, lambda x, y, c: (x, y, c ^ 1))
    from_1 = moved(own, lambda x, y, c: (x + 1, y, c))
    from_2 = moved(own, lambda x, y, c: (x + 2, y, c))

    meta, parts, side, gain, pieces, *state = attend(
        [
            here.reshape(1),
            lax.axis_index("branch").reshape(1),
            norm_gain,
            head_weight,
            segments.reshape(-1, HD),
            q,
        ],
        [own],
        ((1, 0, 0, 0),),
    )
    column = jnp.concatenate([from_2, from_1, own])
    pick = lambda up: jnp.where(up, column[1:], column[:2])
    across_2 = moved(pick(y < 2), lambda x, y, c: (x, y ^ 2, c))
    across_1 = moved(pick((y & 1) == 0), lambda x, y, c: (x, y ^ 1, c))
    column_p = partner(column)
    state = attend(
        [meta, parts], [column, column_p], ((2, -2, 0, 0), (3, -2, 0, 1)), state
    )
    state = attend([meta, parts], [across_1], ((2, None, 1, 0),), state)
    across_3 = moved(across_2, lambda x, y, c: (x, y ^ 1, c))
    near = jnp.concatenate([across_1, across_2])
    near_p = partner(near)
    state = attend([meta, parts], [across_2], ((2, None, 2, 0),), state)
    state = attend([meta, parts], [near_p], ((4, None, (1, 2), 1),), state)
    across_3p = partner(across_3)
    state = attend([meta, parts], [across_3], ((2, None, 3, 0),), state)
    branches = lax.axis_size("branch")
    members = branches * lax.axis_size("tp")
    scaled, stats = attend(
        [meta, parts], [across_3p], ((2, None, 3, 1),), state, (gain, pieces), members
    )
    everyone = lax.all_to_all(stats, ("branch", "tp"), 0, 0, tiled=True)
    normed, joined = pl.pallas_call(
        functools.partial(finish_kernel, branches),
        out_shape=(
            jax.ShapeDtypeStruct((rows, width), jnp.bfloat16),
            jax.ShapeDtypeStruct((1, rows), jnp.float32),
        ),
        in_specs=[VMEM] * 3,
        out_specs=(VMEM,) * 2,
        compiler_params=SMALL,
        name="finish",
    )(side, everyone, scaled)
    return (normed[None], joined[0])


def solution(mesh):
    return jax.shard_map(
        local,
        mesh=mesh,
        in_specs=(
            P("branch", "ctx", "tp"),
            P("branch", "ctx", "tp"),
            P("branch", "ctx", "tp"),
            P(),
            P("branch", "tp"),
            P("branch", "tp"),
        ),
        out_specs=(P("branch", "ctx", "tp"), P("ctx")),
        check_vma=False,
    )
```
